32 devices in a mesh: rep: 4 (over z), fsdp: 2 (over x), seq: 4 (over y, core).
Axes of the slice: x: 2, y: 2, z: 4, core: 2. Of those that a mesh axis runs over, the one named last changes fastest.
Arguments:
- tokens: bfloat16 [8, 1024, 640], P(('rep', 'fsdp'), 'seq'), may hold values from -6 to 6
- d_out: bfloat16 [8, 1024, 640], P(('rep', 'fsdp'), 'seq'), may hold values from -6 to 6
- doc_lengths: int32 [8, 3], P(('rep', 'fsdp')), may hold values from 1 to 640, 1024 in all within a row
- w_query: bfloat16 [640, 1024], P('fsdp'), may hold values from -0.25 to 0.25
- w_key: bfloat16 [640, 256], P('fsdp'), may hold values from -0.25 to 0.25
- w_value: bfloat16 [640, 256], P('fsdp'), may hold values from -0.25 to 0.25
- w_out: bfloat16 [1024, 640], P('fsdp'), may hold values from -0.1875 to 0.1875
- w_gate: bfloat16 [640, 2048], P('fsdp'), may hold values from -0.25 to 0.25
- w_up: bfloat16 [640, 2048], P('fsdp'), may hold values from -0.25 to 0.25
- w_down: bfloat16 [2048, 640], P('fsdp'), may hold values from -0.125 to 0.125
- g_input: bfloat16 [640], P('fsdp'), may hold values from 0.5 to 1.5
- g_query: bfloat16 [256], P('fsdp'), may hold values from 0.25 to 1.75
- g_key: bfloat16 [256], P('fsdp'), may hold values from 0.25 to 1.75
- g_attn: bfloat16 [640], P('fsdp'), may hold values from 0.5 to 1.5
- g_ffin: bfloat16 [640], P('fsdp'), may hold values from 0.5 to 1.5
- g_ffout: bfloat16 [640], P('fsdp'), may hold values from 0.5 to 1.5
Outputs:
- result: bfloat16 [8, 1024, 640], P(('rep', 'fsdp'), 'seq')
- d_tokens: bfloat16 [8, 1024, 640], P(('rep', 'fsdp'), 'seq')
- grad_query: float32 [640, 1024], P('fsdp')
- grad_key: float32 [640, 256], P('fsdp')
- grad_value: float32 [640, 256], P('fsdp')
- grad_out: float32 [1024, 640], P('fsdp')
- grad_gate: float32 [640, 2048], P('fsdp')
- grad_up: float32 [640, 2048], P('fsdp')
- grad_down: float32 [2048, 640], P('fsdp')
- grad_ginput: float32 [640], P('fsdp')
- grad_gquery: float32 [256], P('fsdp')
- grad_gkey: float32 [256], P('fsdp')
- grad_gattn: float32 [640], P('fsdp')
- grad_gffin: float32 [640], P('fsdp')
- grad_gffout: float32 [640], P('fsdp')
The draws below stay inside these ranges and needn't reach their ends.
Inputs may be any that keep to these rules, and one draw needn't show every extreme that they name: `doc_lengths`: each row lists the lengths of the 3 documents packed in order into one sequence; a row sums to 1024 and its largest entry is 640.
All inputs are finite; a program needn't handle non-finite values.
Results may differ from the reference program's by a relative error of at most 0.024.
Values may be sent and summed in bfloat16 or wider, within the bound.
A program may use at most 128 MiB of HBM per device.

```python
import math
import jax
import jax.numpy as jnp
import numpy as np
from jax import lax

D = 640
HEADS = 4
HD = 256
FF = 2048
NDOC = 3
SEQ_LEN = 1024
SEQS_ALL = 8
MAX_DOC = 640


def levels(rng, dims, split, smallest, high):
    def one(dim, parts):
        heights = jax.random.uniform(jax.random.fold_in(jax.random.fold_in(rng, 6), dim), (parts,), jnp.float32, smallest / len(split), high / len(split))
        return jnp.repeat(jnp.exp(heights), dims[dim] // parts).reshape((-1,) + (1,) * (len(dims) - dim - 1))

    loudness = one(*split[0])
    for cut in split[1:]:
        loudness = loudness * one(*cut)
    return loudness


def split_up(count, total, limit, lean):
    loads = [(1 << 20) // math.isqrt(grade ** lean) + 1 for grade in range(2, count + 1)]
    spare, given = total - limit - (count - 1), [1] * (count - 1)
    while spare > 0:
        candidates = [i for i in range(count - 1) if given[i] < limit]
        whole, left = sum([loads[i] for i in candidates]), spare
        for i in candidates:
            addition = min(limit - given[i], max(1, left * loads[i] // whole), spare)
            given[i] = given[i] + addition
            spare = spare - addition
    return np.array([limit] + given)


def uneven(rng, count, total, reach, skew):
    if count == 2:
        one = jax.random.randint(rng, (), max(1, total - reach), min(reach, total - 1) + 1)
        return jnp.stack([one, total - one])
    lengths = jnp.asarray(split_up(count, total, reach, skew), jnp.int32)
    twos = (count - 1) // 2
    donor, receiver = lengths[1:1 + 2 * twos:2], lengths[2:2 + 2 * twos:2]
    margin = jnp.minimum(donor - 1, reach - receiver)
    moved = jax.random.randint(jax.random.fold_in(rng, 1), (twos,), 0, 1 << 20) % (margin + 1)
    lengths = lengths.at[1:1 + 2 * twos:2].set(donor - moved).at[2:2 + 2 * twos:2].set(receiver + moved)
    return lengths[jax.random.permutation(jax.random.fold_in(rng, 2), count)]


def noise(own_key, extent, deviation, reach, split=(), held_as=jnp.bfloat16):
    loudness = levels(own_key, extent, split, -0.22, 0.18) if split else 1.0
    entries = jax.random.normal(own_key, extent, jnp.float32) * deviation * loudness
    return jnp.minimum(jnp.maximum(entries, -reach), reach).astype(held_as)


def setup_inputs(seed: int = 0) -> dict:
    streams_of = jax.random.split(jax.random.key(seed), 17)
    tokens = noise(streams_of[0], (SEQS_ALL, SEQ_LEN, D), 1.0, 6.0, ((0, 8), (1, 4)))
    d_out = noise(streams_of[1], (SEQS_ALL, SEQ_LEN, D), 1.0, 6.0, ((0, 8), (1, 4)))
    doc_lengths = jax.vmap(lambda own: uneven(own, NDOC, SEQ_LEN, MAX_DOC, 0))(jax.random.split(streams_of[2], SEQS_ALL)).reshape((SEQS_ALL, NDOC)).astype(jnp.int32)
    w_query = noise(streams_of[3], (D, HEADS * HD), D ** -0.5, 0.25, ((0, 2),))
    w_key = noise(streams_of[4], (D, HD), D ** -0.5, 0.25, ((0, 2),))
    w_value = noise(streams_of[5], (D, HD), D ** -0.5, 0.25, ((0, 2),))
    w_out = noise(streams_of[6], (HEADS * HD, D), (HEADS * HD) ** -0.5, 0.1875, ((0, 2),))
    w_gate = noise(streams_of[7], (D, FF), D ** -0.5, 0.25, ((0, 2),))
    w_up = noise(streams_of[8], (D, FF), D ** -0.5, 0.25, ((0, 2),))
    w_down = noise(streams_of[9], (FF, D), FF ** -0.5, 0.125, ((0, 2),))
    g_input = jnp.clip(1.0 + 0.1 * jax.random.normal(streams_of[10], (D,), jnp.float32), 0.5, 1.5).astype(jnp.bfloat16)
    g_query = jnp.clip(1.0 + 0.15 * jax.random.normal(streams_of[11], (HD,), jnp.float32), 0.25, 1.75).astype(jnp.bfloat16)
    g_key = jnp.clip(1.0 + 0.15 * jax.random.normal(streams_of[12], (HD,), jnp.float32), 0.25, 1.75).astype(jnp.bfloat16)
    g_attn = jnp.clip(1.0 + 0.1 * jax.random.normal(streams_of[13], (D,), jnp.float32), 0.5, 1.5).astype(jnp.bfloat16)
    g_ffin = jnp.clip(1.0 + 0.1 * jax.random.normal(streams_of[14], (D,), jnp.float32), 0.5, 1.5).astype(jnp.bfloat16)
    g_ffout = jnp.clip(1.0 + 0.1 * jax.random.normal(streams_of[15], (D,), jnp.float32), 0.5, 1.5).astype(jnp.bfloat16)
    return dict(tokens=tokens, d_out=d_out, doc_lengths=doc_lengths, w_query=w_query, w_key=w_key, w_value=w_value, w_out=w_out, w_gate=w_gate, w_up=w_up, w_down=w_down, g_input=g_input, g_query=g_query, g_key=g_key, g_attn=g_attn, g_ffin=g_ffin, g_ffout=g_ffout)


EPS = 1e-06
ROPE_BASE = 1000000.0
MASKED = -1e+30
HIGH = lax.Precision.HIGHEST

@jax.custom_vjp
def low(v):
    return lax.optimization_barrier(v.astype(jnp.bfloat16)).astype(jnp.float32)

@jax.custom_vjp
def low_back(v):
    return v

def low_keep(v):
    return (low(v), None)

def low_pass(kept, grad):
    return (grad,)

def back_keep(v):
    return (v, None)

def back_low(kept, grad):
    return (low(grad),)
low.defvjp(low_keep, low_pass)
low_back.defvjp(back_keep, back_low)

def rms_norm(values, gain_vec):
    return values * lax.rsqrt(lax.optimization_barrier(jnp.mean(values * values, axis=-1, keepdims=True)) + EPS) * gain_vec

def rotate(values, angles):
    half_width = values.shape[-1] // 2
    front_half = values[..., :half_width]
    back_half = values[..., half_width:]
    cos_part = jnp.cos(angles)
    sin_part = jnp.sin(angles)
    return jnp.concatenate([front_half * cos_part - back_half * sin_part, back_half * cos_part + front_half * sin_part], axis=-1)

def frequencies(head_size):
    return jnp.power(jnp.float32(ROPE_BASE), -2.0 * jnp.arange(head_size // 2, dtype=jnp.float32) / head_size)

def layout(lengths_row, total_len):
    doc_ends = jnp.cumsum(lengths_row).astype(jnp.int32)
    starts = (doc_ends - lengths_row).astype(jnp.int32)
    indices = jnp.arange(total_len, dtype=jnp.int32)
    segment = lax.optimization_barrier(jnp.sum((indices[:, None] >= doc_ends[None, :]).astype(jnp.int32), axis=1)).astype(jnp.int32)
    onehot = segment[:, None] == jnp.arange(lengths_row.shape[0], dtype=jnp.int32)[None, :]
    doc_begin = lax.optimization_barrier(jnp.sum(jnp.where(onehot, starts[None, :], 0), axis=1)).astype(jnp.int32)
    return (segment, (indices - doc_begin).astype(jnp.int32))

def matmul(left_side, right_side):
    return jnp.dot(left_side, right_side, precision=HIGH)

def gelu_tanh(values):
    return jax.nn.gelu(values, approximate=True)

def sequence_forward(params, inputs, segment, position):
    w_query, w_key, w_value, w_out, w_gate, w_up, w_down, g_input, g_query, g_key, g_attn, g_ffin, g_ffout = params
    length = inputs.shape[0]
    angles = position.astype(jnp.float32)[:, None] * frequencies(HD)[None, :]
    attn_in = low(rms_norm(inputs, g_input))
    q_proj = low_back(matmul(attn_in, w_query))
    k_proj = low_back(matmul(attn_in, w_key))
    values = low(low_back(matmul(attn_in, w_value)))
    queries = low(rotate(rms_norm(q_proj.reshape(length, HEADS, HD), g_query), angles[:, None, :]))
    keys = low(rotate(rms_norm(k_proj, g_key), angles))
    raw_scores = low_back(jnp.einsum('shd,td->sht', queries, keys, precision=HIGH))
    places = jnp.arange(length, dtype=jnp.int32)
    allowed = (segment[:, None] == segment[None, :]) & (places[:, None] >= places[None, :])
    scores = jnp.where(allowed[:, None, :], raw_scores * HD ** (-0.5), MASKED)
    top_score = lax.optimization_barrier(jnp.max(scores, axis=-1, keepdims=True))
    shifted = jnp.exp(scores - top_score)
    probs = low(shifted / lax.optimization_barrier(jnp.sum(shifted, axis=-1, keepdims=True)))
    mixed = jnp.einsum('sht,td->shd', probs, values, precision=HIGH).reshape(length, HEADS * HD)
    mixed = low(low_back(mixed))
    out_proj = low_back(matmul(mixed, w_out))
    hidden_one = inputs + rms_norm(out_proj, g_attn)
    ff_in = low(rms_norm(hidden_one, g_ffin))
    gate_proj = low_back(matmul(ff_in, w_gate))
    up_proj = low_back(matmul(ff_in, w_up))
    hidden = low(gelu_tanh(gate_proj) * up_proj)
    down_proj = low_back(matmul(hidden, w_down))
    return hidden_one + rms_norm(down_proj, g_ffout)

def reference(tokens, d_out, doc_lengths, w_query, w_key, w_value, w_out, w_gate, w_up, w_down, g_input, g_query, g_key, g_attn, g_ffin, g_ffout):
    params = tuple((entry.astype(jnp.float32) for entry in (w_query, w_key, w_value, w_out, w_gate, w_up, w_down, g_input, g_query, g_key, g_attn, g_ffin, g_ffout)))
    segment, position = jax.vmap(lambda lengths_row: layout(lengths_row, SEQ_LEN))(doc_lengths)

    def forward(weights, inputs):
        per_sequence = jax.checkpoint(lambda element: sequence_forward(weights, element[0], element[1], element[2]))
        return lax.map(per_sequence, (inputs, segment, position))
    result, pullback = jax.vjp(forward, params, tokens.astype(jnp.float32))
    grads, d_inputs = pullback(d_out.astype(jnp.float32))
    return (result.astype(jnp.bfloat16), d_inputs.astype(jnp.bfloat16), grads[0], grads[1], grads[2], grads[3], grads[4], grads[5], grads[6], grads[7], grads[8], grads[9], grads[10], grads[11], grads[12])
```

```python
import jax
import jax.numpy as jnp
from jax import lax
from jax.sharding import PartitionSpec as P

EPS = 1e-06
ROPE_BASE = 1000000.0
MASKED = -1e30


def rms_norm(values, gain_vec):
    return values * lax.rsqrt(jnp.mean(values * values, axis=-1, keepdims=True) + EPS) * gain_vec


def rotate(values, angles):
    half_width = values.shape[-1] // 2
    front_half = values[..., :half_width]
    back_half = values[..., half_width:]
    cos_part = jnp.cos(angles)
    sin_part = jnp.sin(angles)
    return jnp.concatenate(
        [
            front_half * cos_part - back_half * sin_part,
            back_half * cos_part + front_half * sin_part,
        ],
        axis=-1,
    )


def frequencies(head_size):
    return jnp.power(
        jnp.float32(ROPE_BASE), -2.0 * jnp.arange(head_size // 2, dtype=jnp.float32) / head_size
    )


def layout(lengths_row, total_len):
    doc_ends = jnp.cumsum(lengths_row)
    starts = doc_ends - lengths_row
    indices = jnp.arange(total_len, dtype=jnp.int32)
    segment = jnp.sum((indices[:, None] >= doc_ends[None, :]).astype(jnp.int32), axis=1)
    onehot = segment[:, None] == jnp.arange(lengths_row.shape[0], dtype=jnp.int32)[None, :]
    doc_begin = jnp.sum(jnp.where(onehot, starts[None, :], 0), axis=1)
    return (segment, indices - doc_begin)


def matmul(left_side, right_side):
    return jnp.dot(left_side, right_side, preferred_element_type=jnp.float32)


def times_transpose(left_side, right_side):
    return lax.dot_general(
        left_side, right_side, (((1,), (1,)), ((), ())), preferred_element_type=jnp.float32
    )


def transpose_times(left_side, right_side):
    return lax.dot_general(
        left_side, right_side, (((0,), (0,)), ((), ())), preferred_element_type=jnp.float32
    )


def gated(gate_proj, up_proj):
    return jax.nn.gelu(gate_proj, approximate=True) * up_proj


def swap(values, axis_name, bit):
    size = lax.axis_size(axis_name)
    return lax.ppermute(values, axis_name, [(i, i ^ bit) for i in range(size)])


def halve(values, axis_name, bit, dim):
    mine = (lax.axis_index(axis_name) // bit) % 2
    sent = lax.dynamic_index_in_dim(values, 1 - mine, dim, keepdims=False)
    kept = lax.dynamic_index_in_dim(values, mine, dim, keepdims=False)
    arrived = swap(sent, axis_name, bit)
    return (kept.astype(jnp.float32) + arrived.astype(jnp.float32)).astype(jnp.bfloat16)


def paired():
    return lax.axis_size("fsdp") == 2 and lax.axis_size("seq") == 4


def gather_rows(shard):
    if not paired():
        return lax.all_gather(shard, "fsdp", axis=0, tiled=True)
    rows = shard.shape[0] // 4
    piece = lax.dynamic_slice_in_dim(shard, lax.axis_index("seq") * rows, rows)
    other = lax.all_gather(swap(piece, "fsdp", 1), "seq", axis=0, tiled=True)
    first = lax.axis_index("fsdp") == 0
    return jnp.concatenate([jnp.where(first, shard, other), jnp.where(first, other, shard)], axis=0)


def reduce_blocks(blocks, across_first, before):
    _, _, rows, columns = blocks.shape
    part = blocks.reshape(2, 2, 2, rows, columns)
    part = halve(part, "seq", 1, 2)
    if across_first:
        part = halve(part, "fsdp", 1, 0)
        part = halve(part, "seq", 2, 0)
    else:
        part = halve(part, "seq", 2, 1)
        part = halve(part, "fsdp", 1, 0)
    if before is not None:
        part, _ = lax.optimization_barrier((part, before))
    part = lax.psum(part, "rep")
    return lax.all_gather(part, "seq", axis=0, tiled=True).reshape(4, rows, columns), part


def reduce_rows(grad, across_first, before):
    low = grad.astype(jnp.bfloat16)
    if not paired():
        own = lax.psum_scatter(low, "fsdp", scatter_dimension=0, tiled=True)
        return lax.psum(own, ("rep", "seq")).astype(jnp.float32), None
    rows, columns = low.shape
    own, last = reduce_blocks(low.reshape(2, 4, rows // 8, columns), across_first, before)
    return own.reshape(rows // 2, columns).astype(jnp.float32), last


def reduce_with_gains(grad, gains, before):
    width = gains.shape[1]
    rows, columns = grad.shape
    if not paired() or width > columns:
        own = lax.psum_scatter(
            gains.astype(jnp.bfloat16), "fsdp", scatter_dimension=0, tiled=True
        )
        own = lax.psum(own, ("rep", "seq")).astype(jnp.float32)
        return reduce_rows(grad, True, before)[0], own[0]
    extra = jnp.pad(
        gains.astype(jnp.bfloat16)[:, None, None, :],
        ((0, 0), (0, 3), (0, 15), (0, columns - width)),
    )
    blocks = jnp.concatenate(
        [grad.astype(jnp.bfloat16).reshape(2, 4, rows // 8, columns), extra], axis=2
    )
    own, _ = reduce_blocks(blocks, True, before)
    matrix = own[:, : rows // 8].reshape(rows // 2, columns).astype(jnp.float32)
    return matrix, own[0, rows // 8, :width].astype(jnp.float32)


def body(
    tokens,
    d_out,
    doc_lengths,
    w_query,
    w_key,
    w_value,
    w_out,
    w_gate,
    w_up,
    w_down,
    g_input,
    g_query,
    g_key,
    g_attn,
    g_ffin,
    g_ffout,
):
    shards = lax.axis_size("fsdp")
    gain_shards = (g_input, g_query, g_key, g_attn, g_ffin, g_ffout)
    widths = [entry.shape[0] for entry in gain_shards]
    starts = [sum(widths[:i]) for i in range(len(widths))]
    gain_rows = lax.all_gather(jnp.concatenate(gain_shards)[None], "fsdp", axis=0, tiled=True)
    gain_input, gain_query, gain_key, gain_attn, gain_ffin, gain_ffout = [
        gain_rows[:, at : at + width].reshape(-1).astype(jnp.float32)
        for at, width in zip(starts, widths)
    ]
    qkv_mat = gather_rows(jnp.concatenate([w_query, w_key, w_value], axis=1))
    out_mat = gather_rows(w_out)
    gate_up_mat = gather_rows(jnp.concatenate([w_gate, w_up], axis=1))
    down_mat = gather_rows(w_down)
    row_count = tokens.shape[1]
    head_size = gain_query.shape[0]
    query_width = w_query.shape[1]
    head_count = query_width // head_size
    ff_width = w_gate.shape[1]
    total_len = row_count * lax.axis_size("seq")
    segment, position = layout(doc_lengths[0], total_len)
    offset = lax.axis_index("seq") * row_count
    query_seg = lax.dynamic_slice_in_dim(segment, offset, row_count)
    query_pos = lax.dynamic_slice_in_dim(position, offset, row_count)
    places = offset + jnp.arange(row_count, dtype=jnp.int32)
    allowed = (query_seg[:, None] == segment[None, :]) & (
        places[:, None] >= jnp.arange(total_len, dtype=jnp.int32)[None, :]
    )
    angles = query_pos.astype(jnp.float32)[:, None] * frequencies(head_size)[None, :]
    scaling = head_size ** (-0.5)
    inputs = tokens[0].astype(jnp.float32)
    cotangent = d_out[0].astype(jnp.float32)
    input_norm, input_pull = jax.vjp(rms_norm, inputs, gain_input)
    attn_input = input_norm.astype(jnp.bfloat16)
    qkv_proj = matmul(attn_input, qkv_mat)
    q_proj = qkv_proj[:, :query_width]
    k_proj = qkv_proj[:, query_width : query_width + head_size]
    v_proj = qkv_proj[:, query_width + head_size :]

    def query_fn(projected, gain_vec):
        shaped = projected.reshape(projected.shape[0], -1, gain_vec.shape[0])
        return rotate(rms_norm(shaped, gain_vec), angles[:, None, :])

    def key_fn(projected, gain_vec):
        return rotate(rms_norm(projected, gain_vec), angles)

    queries, query_pull = jax.vjp(query_fn, q_proj, gain_query)
    keys_own, key_pull = jax.vjp(key_fn, k_proj, gain_key)
    query_rows = queries.astype(jnp.bfloat16).reshape(row_count * head_count, head_size)
    key_value_rows = lax.all_gather(
        jnp.concatenate([keys_own.astype(jnp.bfloat16), v_proj.astype(jnp.bfloat16)], axis=1),
        "seq",
        axis=0,
        tiled=True,
    )
    key_rows = key_value_rows[:, :head_size]
    value_rows = key_value_rows[:, head_size:]

    def masked_scores():
        raw_scores = times_transpose(query_rows, key_rows).reshape(row_count, head_count, total_len)
        return jnp.where(allowed[:, None, :], raw_scores * scaling, MASKED)

    scores = masked_scores()
    top_score = jnp.max(scores, axis=-1, keepdims=True)
    shifted = jnp.exp(scores - top_score)
    denominator = jnp.sum(shifted, axis=-1, keepdims=True)
    log_total = top_score + jnp.log(denominator)
    probs_low = (
        (shifted / denominator).astype(jnp.bfloat16).reshape(row_count * head_count, total_len)
    )
    mixed_rows = (
        matmul(probs_low, value_rows)
        .reshape(row_count, head_count * head_size)
        .astype(jnp.bfloat16)
    )
    out_proj = matmul(mixed_rows, out_mat)
    attn_norm, attn_pull = jax.vjp(rms_norm, out_proj, gain_attn)
    hidden_one = inputs + attn_norm
    ffin_norm, ffin_pull = jax.vjp(rms_norm, hidden_one, gain_ffin)
    ff_input = ffin_norm.astype(jnp.bfloat16)
    gate_up_proj = matmul(ff_input, gate_up_mat)
    gate_proj = gate_up_proj[:, :ff_width]
    up_proj = gate_up_proj[:, ff_width:]
    activated, gated_pull = jax.vjp(gated, gate_proj, up_proj)
    hidden = activated.astype(jnp.bfloat16)
    down_proj = matmul(hidden, down_mat)
    ffout_norm, ffout_pull = jax.vjp(rms_norm, down_proj, gain_ffout)
    result = hidden_one + ffout_norm
    d_down, grad_gffout = ffout_pull(cotangent)
    d_down_low = d_down.astype(jnp.bfloat16)
    total_down, last = reduce_rows(transpose_times(hidden, d_down_low), True, None)
    d_hidden = times_transpose(d_down_low, down_mat)
    d_gate, d_up = gated_pull(d_hidden)
    d_gate_up_low = jnp.concatenate(
        [d_gate.astype(jnp.bfloat16), d_up.astype(jnp.bfloat16)], axis=1
    )
    total_gate_up, last = reduce_rows(transpose_times(ff_input, d_gate_up_low), False, last)
    d_ffin = times_transpose(d_gate_up_low, gate_up_mat)
    d_hidden_part, grad_gffin = ffin_pull(d_ffin)
    d_hidden_one = cotangent + d_hidden_part
    d_out_proj, grad_gattn = attn_pull(d_hidden_one)
    d_out_low = d_out_proj.astype(jnp.bfloat16)
    total_out, last = reduce_rows(transpose_times(mixed_rows, d_out_low), True, last)
    d_mixed = (
        times_transpose(d_out_low, out_mat)
        .astype(jnp.bfloat16)
        .reshape(row_count * head_count, head_size)
    )
    probs_full = jnp.exp(masked_scores() - log_total)
    d_probs = times_transpose(d_mixed, value_rows).reshape(row_count, head_count, total_len)
    row_dot = jnp.sum(probs_full * d_probs, axis=-1, keepdims=True)
    d_raw = (
        (probs_full * (d_probs - row_dot) * scaling)
        .astype(jnp.bfloat16)
        .reshape(row_count * head_count, total_len)
    )
    grad_rows = jnp.concatenate(
        [
            transpose_times(d_raw, query_rows).astype(jnp.bfloat16),
            transpose_times(probs_low, d_mixed).astype(jnp.bfloat16),
        ],
        axis=1,
    )
    d_queries = matmul(d_raw, key_rows).reshape(row_count, head_count, head_size)
    if paired():
        grad_own = grad_rows.reshape(2, 2, row_count, 2 * head_size)
        grad_own = halve(halve(grad_own, "seq", 1, 1), "seq", 2, 0).astype(jnp.float32)
    else:
        grad_own = lax.psum_scatter(
            grad_rows, "seq", scatter_dimension=0, tiled=True
        ).astype(jnp.float32)
    d_q_proj, grad_gquery = query_pull(d_queries)
    d_k_proj, grad_gkey = key_pull(grad_own[:, :head_size])
    d_qkv_low = jnp.concatenate(
        [
            d_q_proj.astype(jnp.bfloat16),
            d_k_proj.astype(jnp.bfloat16),
            grad_own[:, head_size:].astype(jnp.bfloat16),
        ],
        axis=1,
    )
    d_qkv_low, last, total_down = lax.optimization_barrier((d_qkv_low, last, total_down))
    grad_qkv = transpose_times(attn_input, d_qkv_low)
    d_attn_input = times_transpose(d_qkv_low, qkv_mat)
    d_inputs_part, grad_ginput = input_pull(d_attn_input)
    d_inputs = d_hidden_one + d_inputs_part
    grad_gains = (grad_ginput, grad_gquery, grad_gkey, grad_gattn, grad_gffin, grad_gffout)
    packed_gains = jnp.concatenate([entry.reshape(shards, -1) for entry in grad_gains], axis=1)
    total_qkv, total_gains = reduce_with_gains(grad_qkv, packed_gains, last)
    return (
        result.astype(jnp.bfloat16)[None],
        d_inputs.astype(jnp.bfloat16)[None],
        total_qkv[:, :query_width],
        total_qkv[:, query_width : query_width + head_size],
        total_qkv[:, query_width + head_size :],
        total_out,
        total_gate_up[:, :ff_width],
        total_gate_up[:, ff_width:],
        total_down,
    ) + tuple(total_gains[at : at + width] for at, width in zip(starts, widths))


def solution(mesh):
    in_specs = (
        P(("rep", "fsdp"), "seq", None),
        P(("rep", "fsdp"), "seq", None),
        P(("rep", "fsdp"), None),
        P("fsdp", None),
        P("fsdp", None),
        P("fsdp", None),
        P("fsdp", None),
        P("fsdp", None),
        P("fsdp", None),
        P("fsdp", None),
        P("fsdp"),
        P("fsdp"),
        P("fsdp"),
        P("fsdp"),
        P("fsdp"),
        P("fsdp"),
    )
    out_specs = (
        P(("rep", "fsdp"), "seq", None),
        P(("rep", "fsdp"), "seq", None),
        P("fsdp", None),
        P("fsdp", None),
        P("fsdp", None),
        P("fsdp", None),
        P("fsdp", None),
        P("fsdp", None),
        P("fsdp", None),
        P("fsdp"),
        P("fsdp"),
        P("fsdp"),
        P("fsdp"),
        P("fsdp"),
        P("fsdp"),
    )
    return jax.shard_map(body, mesh=mesh, in_specs=in_specs, out_specs=out_specs, check_vma=False)
```
